32 devices in a mesh: row: 4 (over y, core), col: 4 (over z), layer: 2 (over x).
Axes of the slice: x: 2, y: 2, z: 4, core: 2. Of those that a mesh axis runs over, the one named last changes fastest.
Arguments:
- density_blocks: float32 [4, 128, 2, 4096], P('row', ('col', 'layer')), may hold values from -0.44 to 0.44, as said below
- density_rows: int32 [4, 128, 2], P('row', ('col', 'layer')), may hold values from -1 to 127, as said below
- pattern_rows: int32 [4, 128, 2], P('row', 'col'), may hold values from -1 to 127, as said below
Outputs:
- purified: float32 [4, 128, 2, 4096], P('row', ('col', 'layer'))
The draws below stay inside these ranges and needn't reach their ends.
Inputs may be any that keep to these rules, and one draw needn't show every extreme that they name: `density_rows`: each entry is -1 or a block row i with i // 32 = g and (i % 32) // 16 = l, where g and l are the entry's first and third indices. Same rule as density_rows; pattern_rows equals density_rows wherever density_rows is not -1. `density_blocks`: zero wherever density_rows is -1.
All inputs are finite; a program needn't handle non-finite values.
Results may differ from the reference program's by a relative error of at most 0.000075.
Values sent between devices are 32-bit elements; how exact they have to be, the bound alone decides.
A program may use at most 192 MiB of HBM per device.

```python
import jax
import jax.numpy as jnp
from jax import lax

BS = 64
RB = 32
ROWGROUPS = 4
LSETS = 2
NB = 128
CB = 32
CPD = 16
NCAND = 16


def pattern_draw(key):
    base = jax.random.fold_in(key, 11)
    key_pick, key_dense, key_pattern, key_force = jax.random.split(base, 4)
    groups = ROWGROUPS * NB * LSETS
    picked = jax.random.randint(key_pick, (groups,), 0, NCAND, dtype=jnp.int32)
    live_dense = jax.random.randint(key_dense, (groups,), 0, 2, dtype=jnp.int32)
    forced = jax.random.randint(key_force, (), 0, groups, dtype=jnp.int32)
    live_dense = live_dense.at[forced].set(1)
    extra = jnp.minimum(jax.random.randint(key_pattern, (groups,), 0, 4, dtype=jnp.int32), 1)
    live_pattern = jnp.maximum(live_dense, extra)
    index = jnp.arange(groups, dtype=jnp.int32)
    grid_row = index // (NB * LSETS)
    index_set = index % LSETS
    block_row = grid_row * RB + picked // CPD * CB + index_set * CPD + picked % CPD
    dense_rows = jnp.where(live_dense > 0, block_row, -1).reshape(ROWGROUPS, NB, LSETS)
    pattern_rows = jnp.where(live_pattern > 0, block_row, -1).reshape(ROWGROUPS, NB, LSETS)
    return (dense_rows.astype(jnp.int32), pattern_rows.astype(jnp.int32))


def draw_density_rows(key, part):
    return pattern_draw(key)[0]


def draw_pattern_rows(key, part):
    return pattern_draw(key)[1]


def draw_density_blocks(key, part):
    dense_rows = pattern_draw(key)[0]
    value_key = jax.random.fold_in(key, 23)
    shape = (ROWGROUPS, NB, LSETS, BS * BS)
    values = jnp.clip(0.11 * jax.random.normal(value_key, shape, jnp.float32), -0.44, 0.44)
    return jnp.where((dense_rows >= 0)[..., None], values, 0.0).astype(jnp.float32)


def setup_inputs(seed: int = 0) -> dict:
    key_list = jax.random.split(jax.random.key(seed), 4)
    density_blocks = draw_density_blocks(jax.random.fold_in(key_list[3], 71), 0)
    density_rows = draw_density_rows(jax.random.fold_in(key_list[3], 71), 0)
    pattern_rows = draw_pattern_rows(jax.random.fold_in(key_list[3], 71), 0)
    return dict(density_blocks=density_blocks, density_rows=density_rows, pattern_rows=pattern_rows)


def reference(density_blocks, density_rows, pattern_rows):
    columns = jnp.broadcast_to(jnp.arange(NB, dtype=jnp.int32)[None, :, None], density_rows.shape)
    live_blocks = density_rows >= 0
    safe_rows = jnp.where(live_blocks, density_rows, 0).astype(jnp.int32)
    blocks = jnp.where(live_blocks[..., None], density_blocks, 0.0).reshape(-1, BS, BS)
    grid = jnp.zeros((NB, NB, BS, BS), jnp.float32).at[safe_rows.reshape(-1), columns.reshape(-1)].add(blocks)
    dense = grid.transpose(0, 2, 1, 3).reshape(NB * BS, NB * BS)
    live_pattern = pattern_rows >= 0
    pattern_safe = jnp.where(live_pattern, pattern_rows, 0).astype(jnp.int32)
    keeper = jnp.zeros((NB, NB), jnp.float32).at[pattern_safe.reshape(-1), columns.reshape(-1)].add(
        live_pattern.astype(jnp.float32).reshape(-1))

    def restrict(matrix):
        return (matrix.reshape(NB, BS, NB, BS) * keeper[:, None, :, None]).reshape(NB * BS, NB * BS)

    square = restrict(jnp.dot(dense, dense, precision=lax.Precision.HIGHEST, preferred_element_type=jnp.float32))
    cube = restrict(jnp.dot(dense, square, precision=lax.Precision.HIGHEST, preferred_element_type=jnp.float32))
    mixed = (3.0 * square - 2.0 * cube).reshape(NB, BS, NB, BS).transpose(0, 2, 1, 3)
    picked = mixed[pattern_safe, columns].reshape(ROWGROUPS, NB, LSETS, BS * BS)
    return jnp.where(live_pattern[..., None], picked, 0.0)
```

```python
import jax
import jax.numpy as jnp
from jax import lax
from jax.sharding import PartitionSpec as P

BS = 64


def right_panel(block_values, block_rows):
    moved_values, moved_rows = (
        lax.all_to_all(block_values, "layer", split_axis=2, concat_axis=1, tiled=True),
        lax.all_to_all(block_rows, "layer", split_axis=2, concat_axis=1, tiled=True),
    )
    panel_values, panel_rows = (
        lax.all_gather(moved_values, "row", axis=0, tiled=True),
        lax.all_gather(moved_rows, "row", axis=0, tiled=True),
    )
    return (panel_values[:, :, 0], panel_rows[:, :, 0])


def densify(panel_values, panel_rows, column_keys):
    group_count, block_cols = panel_rows.shape
    width = block_cols * BS
    blocks = jnp.transpose(
        panel_values.reshape(group_count, block_cols, BS, BS), (0, 2, 1, 3)
    ).reshape(group_count, BS, width)
    rows = jnp.repeat(panel_rows, BS, axis=1)
    dense_right = jnp.zeros((column_keys.shape[0], BS, width), jnp.float32)
    for g in range(group_count):
        match = rows[g][None, :] == column_keys[:, None]
        dense_right = jnp.where(match[:, None, :], blocks[g][None], dense_right)
    return dense_right


def fold_panel(left, left_rows, dense_right, local_pattern):
    set_count = left.shape[0]
    block_cols = local_pattern.shape[1]
    panel_cols, _, width = dense_right.shape
    pattern = jnp.repeat(local_pattern, BS, axis=1)
    sums = []
    for l in range(set_count):
        keep = (left_rows[:, l][:, None] == pattern[l][None]) & (pattern[l] >= 0)[None]
        kept = jnp.where(keep[:, None, :], dense_right, 0.0).reshape(panel_cols * BS, width)
        sums.append(jnp.dot(left[l], kept, precision=lax.Precision.HIGH))
    total = jnp.stack(sums).reshape(set_count, BS, block_cols, BS)
    return jnp.transpose(total, (2, 0, 1, 3)).reshape(block_cols, set_count, BS * BS)


def layer_total(partial_sums):
    moved = lax.all_to_all(partial_sums[None], "layer", split_axis=1, concat_axis=0, tiled=True)
    return jnp.sum(moved, axis=0)


def shards(density_blocks, density_rows, pattern_rows):
    layer_count = lax.axis_size("layer")
    layer_index = lax.axis_index("layer")
    per_device = density_blocks.shape[1]
    set_count = density_blocks.shape[2]
    block_cols = per_device * layer_count
    panel_cols = lax.axis_size("col") * per_device
    positions = jnp.arange(panel_cols, dtype=jnp.int32)
    column_keys = (
        positions // per_device * block_cols + layer_index * per_device + positions % per_device
    )
    local_pattern = jnp.transpose(pattern_rows[0], (1, 0))
    own_pattern = lax.dynamic_slice_in_dim(pattern_rows, layer_index * per_device, per_device, 1)
    left_values = lax.all_gather(density_blocks, "col", axis=1, tiled=True)[0]
    left_rows = lax.all_gather(density_rows, "col", axis=1, tiled=True)[0]
    left = jnp.transpose(
        left_values.reshape(panel_cols, set_count, BS, BS), (1, 2, 0, 3)
    ).reshape(set_count, BS, panel_cols * BS)

    def multiply(dense_right):
        return fold_panel(left, left_rows, dense_right, local_pattern)

    first_values, first_rows = right_panel(density_blocks, density_rows)
    square = layer_total(multiply(densify(first_values, first_rows, column_keys)))
    second_values, second_rows = right_panel(square[None], own_pattern)
    cube = layer_total(multiply(densify(second_values, second_rows, column_keys)))
    return (3.0 * square - 2.0 * cube)[None]


def solution(mesh):
    in_specs = (
        P("row", ("col", "layer"), None, None),
        P("row", ("col", "layer"), None),
        P("row", "col", None),
    )
    out_specs = P("row", ("col", "layer"), None, None)
    return jax.shard_map(shards, mesh=mesh, in_specs=in_specs, out_specs=out_specs, check_vma=False)
```
